32 devices in a mesh: seq: 8 (over z, x), chan: 4 (over y, core).
Axes of the slice: x: 2, y: 2, z: 4, core: 2. Of those that a mesh axis runs over, the one named last changes fastest.
Arguments:
- signal: float32 [256, 65536], P('chan', 'seq'), may hold values from -6 to 6
- gating: float32 [256, 65536], P('chan', 'seq'), may hold values from -6 to 6
- response: float32 [256, 65536], P('chan', 'seq'), may hold values from -0.0234375 to 0.0234375
- skip_gain: float32 [256], P('chan'), may hold values from -4 to 4
- mixing_weight: float32 [256, 256], P(None, 'chan'), may hold values from -0.5 to 0.5
Outputs:
- output: float32 [256, 65536], P('chan', 'seq')
The draws below stay inside these ranges and needn't reach their ends.
All inputs are finite; a program needn't handle non-finite values.
Results may differ from the reference program's by a relative error of at most 0.00007.
Values sent between devices are 32-bit elements; how exact they have to be, the bound alone decides.
A program may use at most 128 MiB of HBM per device.

```python
import jax
import jax.numpy as jnp
from jax import lax

D = 256
LENGTH = 65536


def with_spikes(values, own_key, source, target, parts, factor):
    def block_of(position):
        return (jnp.arange(values.shape[position]) // (values.shape[position] // parts)).reshape((-1,) + (1,) * (values.ndim - 1 - position))

    first = jax.random.permutation(own_key, parts)[block_of(target)]
    second = (block_of(target) + parts // 2) % parts
    return jnp.where((block_of(source) == first) | (block_of(source) == second), factor * values, values)


def steps_of(stream_key, shape, shards, least, high):
    loudness = 1.0
    for position, shards_of in shards:
        heights = jax.random.uniform(jax.random.fold_in(jax.random.fold_in(stream_key, 6), position), (shards_of,), jnp.float32, least / len(shards), high / len(shards))
        loudness = loudness * jnp.repeat(jnp.exp(heights), shape[position] // shards_of).reshape((-1,) + (1,) * (len(shape) - 1 - position))
    return loudness


def scatter_about(rng, shape, spread, reach, pieces=(), kind=jnp.bfloat16):
    values = jax.random.normal(rng, shape, jnp.float32) * spread
    if len(pieces) > 0:
        values = steps_of(rng, shape, pieces, -0.22, 0.18) * values
    return jnp.clip(values, min=-reach, max=reach).astype(kind)


def gaussian_with(rng, shape, deviation, most, split, heavy, kind=jnp.bfloat16):
    entries = deviation * jax.random.normal(rng, shape, jnp.float32)
    if split:
        entries = entries * steps_of(rng, shape, split, -0.22, 0.18)
    return jnp.clip(with_spikes(entries, jax.random.fold_in(rng, 3), *heavy), -most, most).astype(kind)


def setup_inputs(seed: int = 0) -> dict:
    keys = jax.random.split(jax.random.key(seed), 6)
    return {
        "signal": scatter_about(keys[0], (D, LENGTH), 1.0, 6.0, ((0, 4), (1, 8)), jnp.float32),
        "gating": scatter_about(keys[1], (D, LENGTH), 1.0, 6.0, ((0, 4), (1, 8)), jnp.float32),
        "response": scatter_about(keys[2], (D, LENGTH), LENGTH ** -0.5, 0.0234375, ((0, 4), (1, 8)), jnp.float32),
        "skip_gain": scatter_about(keys[3], (D,), 1.0, 4.0, ((0, 4),), jnp.float32),
        "mixing_weight": gaussian_with(keys[4], (D, D), D ** -0.5, 0.5, ((1, 4),), (1, 0, 4, 2.0), jnp.float32),
    }


def reference(signal, gating, response, skip_gain, mixing_weight):
    span = signal.shape[1]
    signal_spec = jnp.fft.rfft(signal, n=2 * span, axis=1)
    response_spec = jnp.fft.rfft(response, n=2 * span, axis=1)
    conv = jnp.fft.irfft(signal_spec * response_spec, n=2 * span, axis=1)[:, :span].astype(signal.dtype)
    mixed_in = gating * (conv + skip_gain[:, None] * signal)
    return jnp.dot(mixing_weight, mixed_in, precision=lax.Precision.HIGHEST, preferred_element_type=jnp.float32)
```

```python
from functools import partial
import math

import jax
import jax.numpy as jnp
import numpy as np
from jax import lax
from jax.experimental import pallas as pl
from jax.experimental.pallas import tpu as pltpu
from jax.sharding import PartitionSpec as P

INNER = 256


def halves(table):
    high = np.asarray(table, np.float32).astype(jnp.bfloat16)
    low = (np.asarray(table, np.float64) - high.astype(np.float64)).astype(np.float32).astype(jnp.bfloat16)
    return high, low


def split(value):
    high = value.astype(jnp.bfloat16)
    return high, (value - high.astype(jnp.float32)).astype(jnp.bfloat16)


def tables(span):
    outer = span // INNER
    step_out = np.arange(outer, dtype=np.float64)
    step_in = np.arange(INNER, dtype=np.float64)
    angle = 2 * np.pi * np.mod((4 * step_out[:, None] + 1) * step_out[None, :], 4 * outer) / (4 * outer)
    cos_out, sin_out = np.cos(angle), -np.sin(angle)
    first = np.concatenate(halves(np.concatenate([cos_out, sin_out], axis=0)), axis=1)
    angle = 2 * np.pi * np.mod((4 * step_out[:, None] + 1) * step_in[None, :], 4 * span) / (4 * span)
    twiddle = np.stack([np.cos(angle), -np.sin(angle)]).astype(np.float32)
    angle = 2 * np.pi * np.mod(step_in[:, None] * step_in[None, :], INNER) / INNER
    cos_in, sin_in = np.cos(angle), -np.sin(angle)
    second = np.concatenate(halves(np.block([[cos_in, sin_in], [-sin_in, cos_in]])), axis=0)
    last = np.concatenate(halves(np.concatenate([cos_out.T, -sin_out.T], axis=1) / span), axis=1)
    return first, twiddle, second, last


def matmul(left, right):
    return jnp.dot(left, right, preferred_element_type=jnp.float32)


def table_left(table, value):
    high, low = split(value)
    depth = value.shape[0]
    return matmul(table[...], jnp.concatenate([high, high], axis=0)) + matmul(table[:, :depth], low)


def table_right(value, table):
    high, low = split(value)
    depth = value.shape[1]
    return matmul(jnp.concatenate([high, high], axis=1), table[...]) + matmul(low, table[:depth, :])


def conv_row(signal, response, first, twiddle, second, last):
    outer = signal.shape[0]
    mid = table_left(first, jnp.concatenate([signal, response], axis=1))
    tw_real, tw_imag = twiddle[0], twiddle[1]
    turned = []
    for place in range(2):
        cols = slice(place * INNER, (place + 1) * INNER)
        real, imag = mid[:outer, cols], mid[outer:, cols]
        turned.append(jnp.concatenate(
            [real * tw_real - imag * tw_imag, real * tw_imag + imag * tw_real], axis=1
        ))
    spectra = table_right(jnp.concatenate(turned, axis=0), second)
    s_real, s_imag = spectra[:outer, :INNER], spectra[:outer, INNER:]
    r_real, r_imag = spectra[outer:, :INNER], spectra[outer:, INNER:]
    prod = jnp.concatenate(
        [s_real * r_real - s_imag * r_imag, -(s_real * r_imag + s_imag * r_real)], axis=1
    )
    back = table_right(prod, second)
    real, imag = back[:, :INNER], back[:, INNER:]
    turned = jnp.concatenate(
        [real * tw_real - imag * tw_imag, imag * tw_real + real * tw_imag], axis=0
    )
    return table_left(last, turned)


MESH_ID = pl.DeviceIdType.MESH
WINDOW = 3
AHEAD = 2


def flip(index, mask):
    bit = 1
    while bit <= mask:
        if mask & bit:
            index = index + bit - 2 * bit * ((index // bit) % 2)
        bit *= 2
    return index


def plan(bands):
    upper = (3 * bands) // 8
    up = [("up", k) for k in range(upper)]
    down = [("down", k) for k in range(bands - upper)]
    return upper, up[:2] + down[:1] + up[2:] + down[1:]


def layer_kernel(groups, chans, bands, *refs):
    (signal_h, response_h, gating_h, skip_h, weight_h, first_h, twiddle_h, second_h, last_h, hfirst_h, htwiddle_h, hlast_h,
     out_h,
     signal, response, gating, skip, first, twiddle, second, last, hfirst, htwiddle, hlast,
     send, held, hheld, made, hmade, conv, mixed, wall, wperm, out,
     dn_send, dn_recv, up_send, up_recv, lo_send, lo_recv, dback_send, dback_recv, uback_send, uback_recv,
     sib_send, sib_recv, row_send, row_recv, rel_send, rel_recv, w_send, w_recv, load_sem, out_sem, credit) = refs
    half = groups // 2
    per_band = 8 // half
    n_up, order = plan(bands)
    n_down = bands - n_up
    up_steps, down_steps = n_up * per_band, n_down * per_band
    credits = max(down_steps - WINDOW, 0)
    tiles_in = signal.shape[1]
    samples = tiles_in * 128
    pieces = samples // INNER
    size = 2 * pieces
    chips = chans // 2
    chan_rows = bands * 8
    me = lax.axis_index("seq")
    mine = lax.axis_index("chan")
    chip, core = mine // 2, mine % 2
    sibling = chip * 2 + 1 - core
    low = me < half
    spot = me % half
    out_rows = out.shape[0]
    near = list(range(1, half))
    far = list(range(half, groups))

    def row_band(kind, k):
        return k if kind == "down" else n_down + k

    own_weights = wall.at[pl.ds(pl.multiple_of(mine * chan_rows, 8), chan_rows), :]

    loads = []
    for kind, k in [("down", 0), ("up", 0)] + [("down", k) for k in range(1, n_down)] + [("up", k) for k in range(1, n_up)]:
        b = row_band(kind, k)
        for src, dst in ((signal_h, signal), (response_h, response)):
            loads.append((src.at[b], dst.at[b], b))
    for src, dst in ((first_h, first), (twiddle_h, twiddle), (second_h, second), (last_h, last), (hfirst_h, hfirst),
                     (htwiddle_h, htwiddle), (hlast_h, hlast), (weight_h, own_weights), (skip_h, skip), (gating_h, gating)):
        loads.append((src, dst, -1))
    copies = [(pltpu.make_async_copy(src, dst, load_sem.at[n]), b) for n, (src, dst, b) in enumerate(loads)]

    barrier = pltpu.get_barrier_semaphore()
    for mask in range(1, groups):
        pl.semaphore_signal(barrier, inc=1, device_id={"seq": flip(me, mask)}, device_id_type=MESH_ID)
    for off in range(1, chans):
        pl.semaphore_signal(barrier, inc=1, device_id={"chan": lax.rem(mine + off, chans)}, device_id_type=MESH_ID)
    for copy, _ in copies:
        copy.start()

    def prepare(b):
        for r in range(8):
            for place, ref in enumerate((signal, response)):
                for side in range(2):
                    send[b, r, place, :, side * 128:(side + 1) * 128] = ref[b, pl.ds(side, pieces, stride=2), r, :]

    def source(step, base, who):
        return send.at[base + step // per_band, (step % per_band) * half + who % half]

    def copy_to(src, dst, send_sem, recv_sem, mask):
        return pltpu.make_async_remote_copy(
            src, dst, send_sem, recv_sem, device_id={"seq": flip(me, mask)}, device_id_type=MESH_ID)

    def down(step, mask):
        return copy_to(source(step, 0, flip(me, mask)), held.at[step, me], dn_send.at[step, mask], dn_recv.at[step, mask], mask)

    def down_own(step):
        return pltpu.make_async_copy(source(step, 0, me), held.at[step, me], dn_recv.at[step, 0])

    def up(step, mask):
        return copy_to(source(step, n_down, flip(me, mask)), held.at[step, me], up_send.at[step, mask], up_recv.at[step, mask], mask)

    def up_own(step):
        return pltpu.make_async_copy(source(step, n_down, me), held.at[step, me], up_recv.at[step, 0])

    def lower(step, mask):
        return copy_to(source(step, n_down, flip(me, mask)), hheld.at[step, me], lo_send.at[step, mask], lo_recv.at[step, mask], mask)

    def lower_own(step):
        return pltpu.make_async_copy(source(step, n_down, me), hheld.at[step, me], lo_recv.at[step, 0])

    def made_rows(ref, width, step, who):
        return ref.at[pl.ds(pl.multiple_of((step * width + who) * size, size), size), :]

    def conv_rows(base, step):
        row = (base + step // per_band) * 8 + (step % per_band) * half + spot
        return conv.at[pl.ds(pl.multiple_of(row * size, size), size), :]

    def down_back(step, mask):
        return copy_to(made_rows(made, groups, step, flip(me, mask)), conv_rows(0, step),
                       dback_send.at[step, mask], dback_recv.at[step, mask], mask)

    def down_back_own(step):
        return pltpu.make_async_copy(made_rows(made, groups, step, me), conv_rows(0, step), dback_recv.at[step, 0])

    def up_back(ref, width, step, mask):
        return copy_to(made_rows(ref, width, step, flip(me, mask)), conv_rows(n_down, step),
                       uback_send.at[step, mask], uback_recv.at[step, mask], mask)

    def up_back_own(ref, width, step):
        return pltpu.make_async_copy(made_rows(ref, width, step, me), conv_rows(n_down, step), uback_recv.at[step, 0])

    def convolve(step, lowest):
        rows = held[step]
        result = conv_row(
            rows[:, 0].reshape(groups * pieces, INNER), rows[:, 1].reshape(groups * pieces, INNER),
            first, twiddle, second, last)
        for g in range(lowest, groups):
            for side in range(2):
                start = pl.multiple_of(((step * groups + g) * 2 + side) * pieces, pieces)
                made[pl.ds(start, pieces), :] = result[g * pieces:(g + 1) * pieces, side * 128:(side + 1) * 128]

    def convolve_lower(step):
        rows = hheld[step]
        result = conv_row(
            rows[:, 0].reshape(half * pieces, INNER), rows[:, 1].reshape(half * pieces, INNER),
            hfirst, htwiddle, second, hlast)
        for g in range(half):
            for side in range(2):
                start = pl.multiple_of(((step * half + g) * 2 + side) * pieces, pieces)
                hmade[pl.ds(start, pieces), :] = result[g * pieces:(g + 1) * pieces, side * 128:(side + 1) * 128]

    def chunk(pos, who):
        return mixed.at[pos * chans + who]

    def to_sibling(pos):
        return pltpu.make_async_remote_copy(
            chunk(pos, mine), chunk(pos, mine), sib_send.at[pos], sib_recv.at[pos],
            device_id={"chan": sibling}, device_id_type=MESH_ID)

    def to_chip(pos, off):
        return pltpu.make_async_remote_copy(
            chunk(pos, mine), chunk(pos, mine), row_send.at[pos, off - 1], row_recv.at[pos, off - 1],
            device_id={"chan": lax.rem(chip + off, chips) * 2 + core}, device_id_type=MESH_ID)

    def relay(pos, off):
        who = lax.rem(chip + chips - off, chips) * 2 + core
        return pltpu.make_async_remote_copy(
            chunk(pos, who), chunk(pos, who), rel_send.at[pos, off - 1], rel_recv.at[pos, off - 1],
            device_id={"chan": sibling}, device_id_type=MESH_ID)

    def weights(off):
        return pltpu.make_async_remote_copy(
            own_weights, own_weights, w_send.at[off - 1], w_recv.at[off - 1],
            device_id={"chan": lax.rem(mine + off, chans)}, device_id_type=MESH_ID)

    def gate(pos, is_low):
        kind, k = order[pos]
        b = row_band(kind, k)
        for step in range(k * per_band, (k + 1) * per_band):
            if kind == "down":
                if is_low:
                    down_back_own(step).wait()
                for mask in (near if is_low else far):
                    down_back(step, mask).wait_recv()
            else:
                ref, width = (hmade, half) if is_low else (made, groups)
                up_back_own(ref, width, step).wait()
                for mask in near:
                    up_back(ref, width, step, mask).wait_recv()
        gain = gains[b * 8:(b + 1) * 8]
        for tile in range(tiles_in):
            start = b * 8 * size + (tile % 2) * pieces + tile // 2
            mixed[pos * chans + mine, tile] = gating[b, tile] * (
                conv[pl.ds(start, 8, stride=size), :] + gain * signal[b, tile])
        to_sibling(pos).start()
        for off in range(1, chips):
            to_chip(pos, off).start()

    def pass_on(pos):
        for off in range(1, chips):
            to_chip(pos, off).wait_recv()
            relay(pos, off).start()

    def launch_down(step, is_low):
        for mask in (near if is_low else far):
            down(step, mask).start()
        if is_low:
            down_own(step).start()

    def launch_up(step, is_low):
        for mask in (far if is_low else near):
            up(step, mask).start()
        if is_low:
            for mask in near:
                lower(step, mask).start()
            lower_own(step).start()
        else:
            up_own(step).start()

    def wait_loads(b):
        for copy, which in copies:
            if which == b:
                copy.wait()

    def ready_band(kind, step):
        base = 0 if kind == "down" else n_down
        @pl.when(step % per_band == 0)
        def _():
            prepare(base + step // per_band)

    started = {"down": 0, "up": 0}
    first_steps = {"down": min(WINDOW, down_steps), "up": min(AHEAD, up_steps)}
    for kind, base in (("down", 0), ("up", n_down)):
        for k in range((first_steps[kind] + per_band - 1) // per_band):
            wait_loads(base + k)
            prepare(base + k)
            started[kind] = k + 1
    pl.semaphore_wait(barrier, groups + chans - 2)

    @pl.when(low)
    def _():
        for step in range(max(first_steps.values())):
            if step < first_steps["up"]:
                launch_up(step, True)
            if step < first_steps["down"]:
                launch_down(step, True)

    @pl.when(jnp.logical_not(low))
    def _():
        for step in range(first_steps["down"]):
            launch_down(step, False)
        for step in range(first_steps["up"]):
            launch_up(step, False)

    for kind, base, count in (("down", 0, n_down), ("up", n_down, n_up)):
        for k in range(started[kind], count):
            wait_loads(base + k)
            prepare(base + k)
    wait_loads(-1)
    for off in range(1, chans):
        weights(off).start()
    row = lax.broadcasted_iota(jnp.int32, (chan_rows, chan_rows), 0)
    col = lax.broadcasted_iota(jnp.int32, (chan_rows, chan_rows), 1)
    spread = jnp.where(row == col, jnp.broadcast_to(skip[...], (chan_rows, chan_rows)), 0.0)
    gains = jnp.broadcast_to(jnp.sum(spread, axis=1, keepdims=True), (chan_rows, 128))

    def due(is_low):
        at, rest, m = {}, [], 0
        limit = n_down if is_low else n_up
        for pos, (kind, k) in enumerate(order):
            need = k + 1 if is_low or kind == "up" else 2 * k + 2
            m = max(m, need)
            if m < limit:
                at.setdefault(m, []).append(pos)
            else:
                rest.append(pos)
        return at, rest

    def gates(positions, is_low, previous):
        for pos in positions:
            gate(pos, is_low)
            if previous is not None:
                pass_on(previous)
            previous = pos
        return previous

    def run(is_low):
        at, rest = due(is_low)
        previous = None
        befores = {}
        for m in sorted(at):
            befores[m] = previous
            previous = at[m][-1]
        steps = down_steps if is_low else up_steps

        @pl.loop(0, steps)
        def _(s):
            if is_low:
                down_own(s).wait()
                for mask in near + far:
                    down(s, mask).wait_recv()

                @pl.when(s < credits)
                def _():
                    for mask in far:
                        pl.semaphore_signal(credit.at[s], inc=1, device_id={"seq": flip(me, mask)}, device_id_type=MESH_ID)

                @pl.when(s + AHEAD < up_steps)
                def _():
                    launch_up(s + AHEAD, True)

                @pl.when(s + WINDOW < down_steps)
                def _():
                    launch_down(s + WINDOW, True)

                convolve(s, 0)
                for mask in far + near:
                    down_back(s, mask).start()
                down_back_own(s).start()

                @pl.when(s < up_steps)
                def _():
                    lower_own(s).wait()
                    for mask in near:
                        lower(s, mask).wait_recv()
                    convolve_lower(s)
                    for mask in near:
                        up_back(hmade, half, s, mask).start()
                    up_back_own(hmade, half, s).start()
            else:
                up_own(s).wait()
                for mask in near + far:
                    up(s, mask).wait_recv()

                @pl.when(s + AHEAD < up_steps)
                def _():
                    launch_up(s + AHEAD, False)

                convolve(s, half)
                for mask in near:
                    up_back(made, groups, s, mask).start()
                up_back_own(made, groups, s).start()

                @pl.when(s < credits)
                def _():
                    pl.semaphore_wait(credit.at[s], half)
                    launch_down(s + WINDOW, False)

            for m in sorted(at):
                @pl.when(s == m * per_band)
                def _(m=m):
                    gates(at[m], is_low, befores[m])

        if not is_low:
            for s in range(up_steps, credits):
                pl.semaphore_wait(credit.at[s], half)
                launch_down(s + WINDOW, False)
        previous = gates(rest, is_low, previous)
        pass_on(previous)

        @pl.loop(0, down_steps)
        def _(s):
            for mask in (near if is_low else far):
                down(s, mask).wait_send()
            if is_low:
                for mask in far + near:
                    down_back(s, mask).wait_send()

        @pl.loop(0, up_steps)
        def _(s):
            for mask in (far if is_low else near):
                up(s, mask).wait_send()
            for mask in near:
                if is_low:
                    lower(s, mask).wait_send()
                    up_back(hmade, half, s, mask).wait_send()
                else:
                    up_back(made, groups, s, mask).wait_send()

    @pl.when(low)
    def _():
        run(True)

    @pl.when(jnp.logical_not(low))
    def _():
        run(False)

    for off in range(1, chans):
        weights(off).wait()
    for pos, (kind, k) in enumerate(order):
        for who in range(chans):
            wperm[pl.ds((pos * chans + who) * 8, 8), :] = wall[pl.ds((who * bands + row_band(kind, k)) * 8, 8), :]
    wall[...] = jnp.transpose(wperm[...])
    w_high, w_low = split(wall[pl.ds(pl.multiple_of(mine * out_rows, 8), out_rows), :])
    w_both = jnp.concatenate([w_high, w_low], axis=0)

    @pl.loop(0, bands)
    def _(pos):
        to_sibling(pos).wait()
        for off in range(1, chips):
            to_chip(pos, off).wait_send()
            relay(pos, off).wait()

    depth = chans * chan_rows

    @pl.loop(0, pieces)
    def _(i):
        data = jnp.concatenate([mixed[:, 2 * i + side].reshape(depth, 128) for side in range(2)], axis=1)
        high, low_part = split(data)
        both = matmul(w_both, high)
        out[:, pl.ds(pl.multiple_of(i * INNER, INNER), INNER)] = (
            both[:out_rows] + both[out_rows:] + matmul(w_high, low_part)
        )
    final = pltpu.make_async_copy(out, out_h, out_sem.at[0])
    final.start()
    final.wait()


def tiles(value):
    rows, columns = value.shape
    return value.reshape(rows // 8, 8, columns // 128, 128).transpose(0, 2, 1, 3)


def per_device(signal, gating, response, skip_gain, mixing_weight):
    chan_rows, samples = signal.shape
    groups = lax.axis_size("seq")
    chans = lax.axis_size("chan")
    half = groups // 2
    bands = chan_rows // 8
    per_band = 8 // half
    pieces = samples // INNER
    size = 2 * pieces
    chips = chans // 2
    depth = mixing_weight.shape[0]
    out_rows = depth // chans
    n_up, _ = plan(bands)
    up_steps, down_steps = n_up * per_band, (bands - n_up) * per_band
    slots = max(up_steps, down_steps)
    consts = [jnp.asarray(t) for t in tables(groups * samples)]
    hfirst, htwiddle, _, hlast = [jnp.asarray(t) for t in tables(half * samples)]
    consts += [hfirst, htwiddle, hlast]
    args = [tiles(signal), tiles(response), tiles(gating), skip_gain.reshape(1, chan_rows), mixing_weight.T, *consts]
    f32 = jnp.float32
    sems = pltpu.SemaphoreType.DMA
    anywhere = pl.BlockSpec(memory_space=pl.ANY)
    like = [args[0], args[1], args[2], args[3], *consts]
    n_loads = 2 * bands + len(args) - 2
    return pl.pallas_call(
        partial(layer_kernel, groups, chans, bands),
        in_specs=[anywhere] * len(args),
        out_specs=anywhere,
        out_shape=jax.ShapeDtypeStruct((out_rows, samples), f32),
        scratch_shapes=[pltpu.VMEM(a.shape, a.dtype) for a in like] + [
            pltpu.VMEM((bands, 8, 2, pieces, INNER), f32),
            pltpu.VMEM((slots, groups, 2, pieces, INNER), f32),
            pltpu.VMEM((up_steps, half, 2, pieces, INNER), f32),
            pltpu.VMEM((slots * groups * size, 128), f32),
            pltpu.VMEM((up_steps * half * size, 128), f32),
            pltpu.VMEM((chan_rows * size, 128), f32),
            pltpu.VMEM((bands * chans, samples // 128, 8, 128), f32),
            pltpu.VMEM((chans * chan_rows, depth), f32),
            pltpu.VMEM((chans * chan_rows, depth), f32),
            pltpu.VMEM((out_rows, samples), f32),
            sems((down_steps, groups)), sems((down_steps, groups)),
            sems((up_steps, groups)), sems((up_steps, groups)),
            sems((up_steps, half)), sems((up_steps, half)),
            sems((down_steps, groups)), sems((down_steps, groups)),
            sems((up_steps, half)), sems((up_steps, half)),
            sems((bands,)), sems((bands,)),
            sems((bands, chips - 1)), sems((bands, chips - 1)),
            sems((bands, chips - 1)), sems((bands, chips - 1)),
            sems((chans - 1,)), sems((chans - 1,)),
            sems((n_loads,)), sems((1,)),
            pltpu.SemaphoreType.REGULAR((down_steps,)),
        ],
        compiler_params=pltpu.CompilerParams(
            collective_id=0, has_side_effects=True, vmem_limit_bytes=62 * 2**20
        ),
        name="layer",
    )(*args)


def solution(mesh):
    in_specs = (P("chan", "seq"), P("chan", "seq"), P("chan", "seq"), P("chan"), P(None, "chan"))
    out_specs = P("chan", "seq")
    return jax.shard_map(
        per_device, mesh=mesh, in_specs=in_specs, out_specs=out_specs, check_vma=False
    )
```

```python
from functools import partial
import math

import jax
import jax.numpy as jnp
import numpy as np
from jax import lax
from jax.experimental import pallas as pl
from jax.experimental.pallas import tpu as pltpu
from jax.sharding import PartitionSpec as P

INNER = 256


def halves(table):
    high = np.asarray(table, np.float32).astype(jnp.bfloat16)
    low = (np.asarray(table, np.float64) - high.astype(np.float64)).astype(np.float32).astype(jnp.bfloat16)
    return high, low


def split(value):
    high = value.astype(jnp.bfloat16)
    return high, (value - high.astype(jnp.float32)).astype(jnp.bfloat16)


def tables(span):
    outer = span // INNER
    step_out = np.arange(outer, dtype=np.float64)
    step_in = np.arange(INNER, dtype=np.float64)
    angle = 2 * np.pi * np.mod((4 * step_out[:, None] + 1) * step_out[None, :], 4 * outer) / (4 * outer)
    cos_out, sin_out = np.cos(angle), -np.sin(angle)
    first = np.concatenate(halves(np.concatenate([cos_out, sin_out], axis=0)), axis=1)
    angle = 2 * np.pi * np.mod((4 * step_out[:, None] + 1) * step_in[None, :], 4 * span) / (4 * span)
    twiddle = np.stack([np.cos(angle), -np.sin(angle)]).astype(np.float32)
    angle = 2 * np.pi * np.mod(step_in[:, None] * step_in[None, :], INNER) / INNER
    cos_in, sin_in = np.cos(angle), -np.sin(angle)
    second = np.concatenate(halves(np.block([[cos_in, sin_in], [-sin_in, cos_in]])), axis=0)
    last = np.concatenate(halves(np.concatenate([cos_out.T, -sin_out.T], axis=1) / span), axis=1)
    return first, twiddle, second, last


def matmul(left, right):
    return jnp.dot(left, right, preferred_element_type=jnp.float32)


def table_left(table, value):
    high, low = split(value)
    depth = value.shape[0]
    return matmul(table[...], jnp.concatenate([high, high], axis=0)) + matmul(table[:, :depth], low)


def table_right(value, table):
    high, low = split(value)
    depth = value.shape[1]
    return matmul(jnp.concatenate([high, high], axis=1), table[...]) + matmul(low, table[:depth, :])


def conv_row(signal, response, first, twiddle, second, last):
    outer = signal.shape[0]
    mid = table_left(first, jnp.concatenate([signal, response], axis=1))
    tw_real, tw_imag = twiddle[0], twiddle[1]
    turned = []
    for place in range(2):
        cols = slice(place * INNER, (place + 1) * INNER)
        real, imag = mid[:outer, cols], mid[outer:, cols]
        turned.append(jnp.concatenate(
            [real * tw_real - imag * tw_imag, real * tw_imag + imag * tw_real], axis=1
        ))
    spectra = table_right(jnp.concatenate(turned, axis=0), second)
    s_real, s_imag = spectra[:outer, :INNER], spectra[:outer, INNER:]
    r_real, r_imag = spectra[outer:, :INNER], spectra[outer:, INNER:]
    prod = jnp.concatenate(
        [s_real * r_real - s_imag * r_imag, -(s_real * r_imag + s_imag * r_real)], axis=1
    )
    back = table_right(prod, second)
    real, imag = back[:, :INNER], back[:, INNER:]
    turned = jnp.concatenate(
        [real * tw_real - imag * tw_imag, imag * tw_real + real * tw_imag], axis=0
    )
    return table_left(last, turned)


MESH_ID = pl.DeviceIdType.MESH
WINDOW = 2
AHEAD = 2
LOW_LAG = 1
OUT_PARTS = 4
RELAY_LAG = 2


def flip(index, mask):
    bit = 1
    while bit <= mask:
        if mask & bit:
            index = index + bit - 2 * bit * ((index // bit) % 2)
        bit *= 2
    return index


def plan(bands, per_band):
    upper = (3 * bands) // 8
    lower = bands - upper
    up = [("up", k) for k in range(upper)]
    down = [("down", k) for k in range(lower)]
    on_low, on_high = [], []
    for k in range(lower):
        on_low.append(down[k])
        on_low += up[k:k + 1]
    on_high = up[:2] + down[:1] + up[2:] + down[1:]
    low_steps, high_steps = lower * per_band, upper * per_band
    low_at = [(2 + n) if per_band == 2 else (n + 3) // 2 for n in range(bands)]
    low_at = [at + LOW_LAG if at + LOW_LAG < low_steps else None for at in low_at]
    high_at = [per_band * m for m in (1, 2)] + [high_steps - 1]
    high_at = [high_at[n] if n < len(high_at) else None for n in range(bands)]
    return upper, {True: list(zip(on_low, low_at)), False: list(zip(on_high, high_at))}


def layer_kernel(groups, chans, bands, *refs):
    (signal_h, response_h, gating_h, skip_h, weight_h, first_h, twiddle_h, second_h, last_h, hfirst_h, htwiddle_h, hlast_h,
     out_h,
     signal, response, gating, skip, first, twiddle, second, last, hfirst, htwiddle, hlast,
     send, held, hheld, made, hmade, conv, mixed, wall, wperm, wturn, *shares, out,
     dn_send, dn_recv, up_send, up_recv, lo_send, lo_recv, dback_send, dback_recv, uback_send, uback_recv,
     sib_send, sib_recv, row_send, row_recv, rel_send, rel_recv, w_send, w_recv, load_sem, out_sem, credit) = refs
    half = groups // 2
    per_band = 8 // half
    n_up, orders = plan(bands, per_band)
    n_down = bands - n_up
    cuts = [0, bands // 2, bands - 1, bands]
    up_steps, down_steps = n_up * per_band, n_down * per_band
    credits = max(down_steps - WINDOW, 0)
    tiles_in = signal.shape[1]
    samples = tiles_in * 128
    pieces = samples // INNER
    size = 2 * pieces
    chips = chans // 2
    chan_rows = bands * 8
    me = lax.axis_index("seq")
    mine = lax.axis_index("chan")
    chip, core = mine // 2, mine % 2
    sibling = chip * 2 + 1 - core
    low = me < half
    spot = me % half
    out_rows = out.shape[0]
    near = list(range(1, half))
    far = list(range(half, groups))

    def row_band(kind, k):
        return k if kind == "down" else n_down + k

    own_weights = wall.at[pl.ds(pl.multiple_of(mine * chan_rows, 8), chan_rows), :]

    loads = []
    for kind, k in [("down", 0), ("up", 0)] + [("down", k) for k in range(1, n_down)] + [("up", k) for k in range(1, n_up)]:
        b = row_band(kind, k)
        for src, dst in ((signal_h, signal), (response_h, response)):
            loads.append((src.at[b], dst.at[b], b))
    for src, dst in ((first_h, first), (twiddle_h, twiddle), (second_h, second), (last_h, last), (hfirst_h, hfirst),
                     (htwiddle_h, htwiddle), (hlast_h, hlast), (weight_h, own_weights), (skip_h, skip), (gating_h, gating)):
        loads.append((src, dst, -1))
    copies = [(pltpu.make_async_copy(src, dst, load_sem.at[n]), b) for n, (src, dst, b) in enumerate(loads)]

    barrier = pltpu.get_barrier_semaphore()
    for mask in range(1, groups):
        pl.semaphore_signal(barrier, inc=1, device_id={"seq": flip(me, mask)}, device_id_type=MESH_ID)
    for off in range(1, chans):
        pl.semaphore_signal(barrier, inc=1, device_id={"chan": lax.rem(mine + off, chans)}, device_id_type=MESH_ID)
    for copy, _ in copies:
        copy.start()

    def prepare(b):
        for r in range(8):
            for place, ref in enumerate((signal, response)):
                for side in range(2):
                    send[b, r, place, :, side * 128:(side + 1) * 128] = ref[b, pl.ds(side, pieces, stride=2), r, :]

    def source(step, base, who):
        return send.at[base + step // per_band, (step % per_band) * half + who % half]

    def copy_to(src, dst, send_sem, recv_sem, mask):
        return pltpu.make_async_remote_copy(
            src, dst, send_sem, recv_sem, device_id={"seq": flip(me, mask)}, device_id_type=MESH_ID)

    def down(step, mask):
        return copy_to(source(step, 0, flip(me, mask)), held.at[step * groups + me], dn_send.at[0], dn_recv.at[step], mask)

    def down_own(step):
        return pltpu.make_async_copy(source(step, 0, me), held.at[step * groups + me], dn_recv.at[step])

    def up(step, mask):
        return copy_to(source(step, n_down, flip(me, mask)), held.at[step * groups + me], up_send.at[0], up_recv.at[step], mask)

    def up_own(step):
        return pltpu.make_async_copy(source(step, n_down, me), held.at[step * groups + me], up_recv.at[step])

    def lower(step, mask):
        return copy_to(source(step, n_down, flip(me, mask)), hheld.at[step * half + me], lo_send.at[0], lo_recv.at[step], mask)

    def lower_own(step):
        return pltpu.make_async_copy(source(step, n_down, me), hheld.at[step * half + me], lo_recv.at[step])

    def made_rows(ref, width, step, who):
        return ref.at[pl.ds(pl.multiple_of((step * width + who) * size, size), size), :]

    def conv_rows(base, step):
        row = (base + step // per_band) * 8 + (step % per_band) * half + spot
        return conv.at[pl.ds(pl.multiple_of(row * size, size), size), :]

    def down_back(step, mask):
        return copy_to(made_rows(made, groups, step, flip(me, mask)), conv_rows(0, step),
                       dback_send.at[0], dback_recv.at[step // per_band], mask)

    def down_back_own(step):
        return pltpu.make_async_copy(made_rows(made, groups, step, me), conv_rows(0, step), dback_recv.at[step // per_band])

    def up_back(ref, width, step, mask):
        return copy_to(made_rows(ref, width, step, flip(me, mask)), conv_rows(n_down, step),
                       uback_send.at[0], uback_recv.at[step // per_band], mask)

    def up_back_own(ref, width, step):
        return pltpu.make_async_copy(made_rows(ref, width, step, me), conv_rows(n_down, step), uback_recv.at[step // per_band])

    def settle(ref, sem):
        pltpu.make_async_copy(ref, ref, sem).wait()

    def settle_sent(blocks, rows, sem):
        settle(held.at[pl.ds(0, blocks)] if rows is None else made.at[pl.ds(0, blocks * rows)], sem)

    def convolve(step, lowest):
        rows = held[pl.ds(step * groups, groups)]
        result = conv_row(
            rows[:, 0].reshape(groups * pieces, INNER), rows[:, 1].reshape(groups * pieces, INNER),
            first, twiddle, second, last)
        for g in range(lowest, groups):
            for side in range(2):
                start = pl.multiple_of(((step * groups + g) * 2 + side) * pieces, pieces)
                made[pl.ds(start, pieces), :] = result[g * pieces:(g + 1) * pieces, side * 128:(side + 1) * 128]

    def convolve_lower(step):
        rows = hheld[pl.ds(step * half, half)]
        result = conv_row(
            rows[:, 0].reshape(half * pieces, INNER), rows[:, 1].reshape(half * pieces, INNER),
            hfirst, htwiddle, second, hlast)
        for g in range(half):
            for side in range(2):
                start = pl.multiple_of(((step * half + g) * 2 + side) * pieces, pieces)
                hmade[pl.ds(start, pieces), :] = result[g * pieces:(g + 1) * pieces, side * 128:(side + 1) * 128]

    def chunk(pos, who):
        return mixed.at[pos * chans + who]

    def to_sibling(pos):
        return pltpu.make_async_remote_copy(
            chunk(pos, mine), chunk(pos, mine), sib_send.at[0], sib_recv.at[pos],
            device_id={"chan": sibling}, device_id_type=MESH_ID)

    def to_chip(pos, off):
        return pltpu.make_async_remote_copy(
            chunk(pos, mine), chunk(pos, mine), row_send.at[off - 1], row_recv.at[pos, off - 1],
            device_id={"chan": lax.rem(chip + off, chips) * 2 + core}, device_id_type=MESH_ID)

    def relay(pos, off):
        who = lax.rem(chip + chips - off, chips) * 2 + core
        return pltpu.make_async_remote_copy(
            chunk(pos, who), chunk(pos, who), rel_send.at[off - 1], rel_recv.at[pos, off - 1],
            device_id={"chan": sibling}, device_id_type=MESH_ID)

    def weights(off):
        return pltpu.make_async_remote_copy(
            own_weights, own_weights, w_send.at[off - 1], w_recv.at[off - 1],
            device_id={"chan": lax.rem(mine + off, chans)}, device_id_type=MESH_ID)

    def gate(pos, is_low):
        kind, k = orders[is_low][pos][0]
        b = row_band(kind, k)
        settle(conv.at[pl.ds(b * 8 * size, 8 * size), :], (dback_recv if kind == "down" else uback_recv).at[k])
        gain = gains[b * 8:(b + 1) * 8]
        for tile in range(tiles_in):
            start = b * 8 * size + (tile % 2) * pieces + tile // 2
            mixed[pos * chans + mine, tile] = gating[b, tile] * (
                conv[pl.ds(start, 8, stride=size), :] + gain * signal[b, tile])
        to_sibling(pos).start()
        for off in range(1, chips):
            to_chip(pos, off).start()

    def pass_on(pos):
        for off in range(1, chips):
            to_chip(pos, off).wait_recv()
            relay(pos, off).start()

    def launch_down(step, is_low):
        for mask in (near if is_low else far):
            down(step, mask).start()
        if is_low:
            down_own(step).start()

    def launch_up(step, is_low):
        for mask in (far if is_low else near):
            up(step, mask).start()
        if is_low:
            for mask in near:
                lower(step, mask).start()
            lower_own(step).start()
        else:
            up_own(step).start()

    def wait_loads(b):
        for copy, which in copies:
            if which == b:
                copy.wait()

    def ready_band(kind, step):
        base = 0 if kind == "down" else n_down
        @pl.when(step % per_band == 0)
        def _():
            prepare(base + step // per_band)

    started = {"down": 0, "up": 0}
    first_steps = {"down": min(WINDOW, down_steps), "up": min(AHEAD, up_steps)}
    for kind, base in (("down", 0), ("up", n_down)):
        for k in range((first_steps[kind] + per_band - 1) // per_band):
            wait_loads(base + k)
            prepare(base + k)
            started[kind] = k + 1
    pl.semaphore_wait(barrier, groups + chans - 2)

    @pl.when(low)
    def _():
        for step in range(max(first_steps.values())):
            if step < first_steps["up"]:
                launch_up(step, True)
            if step < first_steps["down"]:
                launch_down(step, True)

    @pl.when(jnp.logical_not(low))
    def _():
        for step in range(first_steps["down"]):
            launch_down(step, False)
        for step in range(first_steps["up"]):
            launch_up(step, False)

    for kind, base, count in (("down", 0, n_down), ("up", n_down, n_up)):
        for k in range(started[kind], count):
            wait_loads(base + k)
            prepare(base + k)
    wait_loads(-1)
    for off in range(1, chans):
        weights(off).start()
    row = lax.broadcasted_iota(jnp.int32, (chan_rows, chan_rows), 0)
    col = lax.broadcasted_iota(jnp.int32, (chan_rows, chan_rows), 1)
    spread = jnp.where(row == col, jnp.broadcast_to(skip[...], (chan_rows, chan_rows)), 0.0)
    gains = jnp.broadcast_to(jnp.sum(spread, axis=1, keepdims=True), (chan_rows, 128))

    def share_weights():
        for off in range(1, chans):
            weights(off).wait()
        for pos in range(bands):
            here = [row_band(*orders[side][pos][0]) for side in (True, False)]
            b = jnp.where(low, here[0], here[1])
            for who in range(chans):
                wperm[pl.ds((pos * chans + who) * 8, 8), :] = wall[
                    pl.ds(pl.multiple_of((who * bands + b) * 8, 8), 8), :]
        for share, (lo, hi) in zip(shares, zip(cuts[:-1], cuts[1:])):
            width = (hi - lo) * chans * 8
            wturn[:, :width] = jnp.transpose(wperm[lo * chans * 8:hi * chans * 8, :])
            w_high, w_low = split(wturn[pl.ds(pl.multiple_of(mine * out_rows, 8), out_rows), :width])
            share[...] = jnp.concatenate([w_high, w_low], axis=0)

    def mix(n):
        lo, hi = cuts[n], cuts[n + 1]
        for pos in range(lo, hi):
            to_sibling(pos).wait_recv()
            for off in range(1, chips):
                relay(pos, off).wait_recv()
        depth = (hi - lo) * chans * 8
        parts = OUT_PARTS if n == len(cuts) - 2 else 1
        for part in range(parts):
            @pl.loop(part * (pieces // parts), (part + 1) * (pieces // parts))
            def _(i):
                data = jnp.concatenate(
                    [mixed[lo * chans:hi * chans, 2 * i + side].reshape(depth, 128) for side in range(2)], axis=1)
                high, low_part = split(data)
                weight_both = shares[n][...]
                both = matmul(weight_both, high)
                here = pl.ds(pl.multiple_of(i * INNER, INNER), INNER)
                total = both[:out_rows] + both[out_rows:] + matmul(weight_both[:out_rows], low_part)
                out[:, here] = total if n == 0 else out[:, here] + total
            if parts > 1:
                here = pl.ds(part * (samples // parts), samples // parts)
                pltpu.make_async_copy(out.at[:, here], out_h.at[:, here], out_sem.at[0]).start()

    def finish():
        for pos in range(bands - RELAY_LAG, bands - 1):
            pass_on(pos)
        mix(1)
        pass_on(bands - 1)
        mix(2)

    def gates(first_pos, last_pos, is_low):
        for pos in range(first_pos, last_pos):
            gate(pos, is_low)
            if pos >= RELAY_LAG:
                pass_on(pos - RELAY_LAG)

    def run(is_low):
        at = [where for _, where in orders[is_low]]
        rest = at.index(None)
        steps = down_steps if is_low else up_steps

        @pl.loop(0, steps)
        def _(s):
            if is_low:
                settle(held.at[pl.ds(s * groups, groups)], dn_recv.at[s])

                @pl.when(s < credits)
                def _():
                    for mask in far:
                        pl.semaphore_signal(credit.at[s], inc=1, device_id={"seq": flip(me, mask)}, device_id_type=MESH_ID)

                @pl.when(s + AHEAD < up_steps)
                def _():
                    launch_up(s + AHEAD, True)

                @pl.when(s + WINDOW < down_steps)
                def _():
                    launch_down(s + WINDOW, True)

                convolve(s, 0)
                down_back_own(s).start()
                for mask in near + far:
                    down_back(s, mask).start()

                @pl.when(s < up_steps)
                def _():
                    settle(hheld.at[pl.ds(s * half, half)], lo_recv.at[s])
                    convolve_lower(s)
                    for mask in near:
                        up_back(hmade, half, s, mask).start()
                    up_back_own(hmade, half, s).start()
            else:
                @pl.when((s > 0) & (s - 1 < credits))
                def _():
                    pl.semaphore_wait(credit.at[s - 1], half)
                    launch_down(s - 1 + WINDOW, False)

                settle(held.at[pl.ds(s * groups, groups)], up_recv.at[s])

                @pl.when(s + AHEAD < up_steps)
                def _():
                    launch_up(s + AHEAD, False)

                convolve(s, half)
                for mask in near:
                    up_back(made, groups, s, mask).start()
                up_back_own(made, groups, s).start()

            @pl.when(s == 1)
            def _():
                share_weights()

            for where in sorted(set(at[:rest])):
                @pl.when(s == where)
                def _(where=where):
                    gates(at.index(where), at.index(where) + at.count(where), is_low)

        if not is_low:
            for s in range(up_steps - 1, credits):
                pl.semaphore_wait(credit.at[s], half)
                launch_down(s + WINDOW, False)
        gates(rest, cuts[2], is_low)
        mix(0)
        sends = ((down_steps * len(near if is_low else far), None, dn_send),
                 (up_steps * len(far if is_low else near), None, up_send),
                 (up_steps * len(near), size, uback_send))
        if is_low:
            sends += ((up_steps * len(near), None, lo_send), (down_steps * len(near + far), size, dback_send))
        gates(cuts[2], bands, is_low)
        finish()
        for blocks, rows, sem in sends:
            settle_sent(blocks, rows, sem.at[0])

    @pl.when(low)
    def _():
        run(True)

    @pl.when(jnp.logical_not(low))
    def _():
        run(False)

    settle(out, out_sem.at[0])
    settle(mixed.at[pl.ds(0, bands)], sib_send.at[0])
    for off in range(1, chips):
        settle(mixed.at[pl.ds(0, bands)], row_send.at[off - 1])
        settle(mixed.at[pl.ds(0, bands)], rel_send.at[off - 1])


def tiles(value):
    rows, columns = value.shape
    return value.reshape(rows // 8, 8, columns // 128, 128).transpose(0, 2, 1, 3)


def per_device(signal, gating, response, skip_gain, mixing_weight):
    chan_rows, samples = signal.shape
    groups = lax.axis_size("seq")
    chans = lax.axis_size("chan")
    half = groups // 2
    bands = chan_rows // 8
    per_band = 8 // half
    pieces = samples // INNER
    size = 2 * pieces
    chips = chans // 2
    depth = mixing_weight.shape[0]
    out_rows = depth // chans
    n_up, _ = plan(bands, per_band)
    up_steps, down_steps = n_up * per_band, (bands - n_up) * per_band
    slots = max(up_steps, down_steps)
    consts = [jnp.asarray(t) for t in tables(groups * samples)]
    hfirst, htwiddle, _, hlast = [jnp.asarray(t) for t in tables(half * samples)]
    consts += [hfirst, htwiddle, hlast]
    args = [tiles(signal), tiles(response), tiles(gating), skip_gain.reshape(1, chan_rows), mixing_weight.T, *consts]
    f32 = jnp.float32
    sems = pltpu.SemaphoreType.DMA
    anywhere = pl.BlockSpec(memory_space=pl.ANY)
    like = [args[0], args[1], args[2], args[3], *consts]
    n_loads = 2 * bands + len(args) - 2
    return pl.pallas_call(
        partial(layer_kernel, groups, chans, bands),
        in_specs=[anywhere] * len(args),
        out_specs=anywhere,
        out_shape=jax.ShapeDtypeStruct((out_rows, samples), f32),
        scratch_shapes=[pltpu.VMEM(a.shape, a.dtype) for a in like] + [
            pltpu.VMEM((bands, 8, 2, pieces, INNER), f32),
            pltpu.VMEM((slots * groups, 2, pieces, INNER), f32),
            pltpu.VMEM((up_steps * half, 2, pieces, INNER), f32),
            pltpu.VMEM((slots * groups * size, 128), f32),
            pltpu.VMEM((up_steps * half * size, 128), f32),
            pltpu.VMEM((chan_rows * size, 128), f32),
            pltpu.VMEM((bands * chans, samples // 128, 8, 128), f32),
            pltpu.VMEM((chans * chan_rows, depth), f32),
            pltpu.VMEM((chans * chan_rows, depth), f32),
            pltpu.VMEM((depth, chans * chan_rows // 2), f32),
            *[pltpu.VMEM((2 * out_rows, n * chans * 8), jnp.bfloat16) for n in (bands // 2, bands // 2 - 1, 1)],
            pltpu.VMEM((out_rows, samples), f32),
            sems((1,)), sems((down_steps,)),
            sems((1,)), sems((up_steps,)),
            sems((1,)), sems((up_steps,)),
            sems((1,)), sems((bands - n_up,)),
            sems((1,)), sems((n_up,)),
            sems((1,)), sems((bands,)),
            sems((chips - 1,)), sems((bands, chips - 1)),
            sems((chips - 1,)), sems((bands, chips - 1)),
            sems((chans - 1,)), sems((chans - 1,)),
            sems((n_loads,)), sems((1,)),
            pltpu.SemaphoreType.REGULAR((down_steps,)),
        ],
        compiler_params=pltpu.CompilerParams(
            collective_id=0, has_side_effects=True, vmem_limit_bytes=62 * 2**20
        ),
        name="layer",
    )(*args)


def solution(mesh):
    in_specs = (P("chan", "seq"), P("chan", "seq"), P("chan", "seq"), P("chan"), P(None, "chan"))
    out_specs = P("chan", "seq")
    return jax.shard_map(
        per_device, mesh=mesh, in_specs=in_specs, out_specs=out_specs, check_vma=False
    )
```

```python
from functools import partial
import math

import jax
import jax.numpy as jnp
import numpy as np
from jax import lax
from jax.experimental import pallas as pl
from jax.experimental.pallas import tpu as pltpu
from jax.sharding import PartitionSpec as P

INNER = 256


def halves(table):
    high = np.asarray(table, np.float32).astype(jnp.bfloat16)
    low = (np.asarray(table, np.float64) - high.astype(np.float64)).astype(np.float32).astype(jnp.bfloat16)
    return high, low


def split(value):
    high = value.astype(jnp.bfloat16)
    return high, (value - high.astype(jnp.float32)).astype(jnp.bfloat16)


def tables(span):
    outer = span // INNER
    step_out = np.arange(outer, dtype=np.float64)
    step_in = np.arange(INNER, dtype=np.float64)
    angle = 2 * np.pi * np.mod((4 * step_out[:, None] + 1) * step_out[None, :], 4 * outer) / (4 * outer)
    cos_out, sin_out = np.cos(angle), -np.sin(angle)
    first = np.concatenate(halves(np.concatenate([cos_out, sin_out], axis=0)), axis=1)
    angle = 2 * np.pi * np.mod((4 * step_out[:, None] + 1) * step_in[None, :], 4 * span) / (4 * span)
    twiddle = np.stack([np.cos(angle), -np.sin(angle)]).astype(np.float32)
    angle = 2 * np.pi * np.mod(step_in[:, None] * step_in[None, :], INNER) / INNER
    cos_in, sin_in = np.cos(angle), -np.sin(angle)
    second = np.concatenate(halves(np.block([[cos_in, sin_in], [-sin_in, cos_in]])), axis=0)
    last = np.concatenate(halves(np.concatenate([cos_out.T, -sin_out.T], axis=1) / span), axis=1)
    return first, twiddle, second, last


def matmul(left, right):
    return jnp.dot(left, right, preferred_element_type=jnp.float32)


def table_left(table, value):
    high, low = split(value)
    depth = value.shape[0]
    return matmul(table[...], jnp.concatenate([high, high], axis=0)) + matmul(table[:, :depth], low)


def table_right(value, table):
    high, low = split(value)
    depth = value.shape[1]
    return matmul(jnp.concatenate([high, high], axis=1), table[...]) + matmul(low, table[:depth, :])


def conv_row(signal, response, first, twiddle, second, last):
    outer = signal.shape[0]
    mid = table_left(first, jnp.concatenate([signal, response], axis=1))
    tw_real, tw_imag = twiddle[0], twiddle[1]
    turned = []
    for place in range(2):
        cols = slice(place * INNER, (place + 1) * INNER)
        real, imag = mid[:outer, cols], mid[outer:, cols]
        turned.append(jnp.concatenate(
            [real * tw_real - imag * tw_imag, real * tw_imag + imag * tw_real], axis=1
        ))
    spectra = table_right(jnp.concatenate(turned, axis=0), second)
    s_real, s_imag = spectra[:outer, :INNER], spectra[:outer, INNER:]
    r_real, r_imag = spectra[outer:, :INNER], spectra[outer:, INNER:]
    prod = jnp.concatenate(
        [s_real * r_real - s_imag * r_imag, -(s_real * r_imag + s_imag * r_real)], axis=1
    )
    back = table_right(prod, second)
    real, imag = back[:, :INNER], back[:, INNER:]
    turned = jnp.concatenate(
        [real * tw_real - imag * tw_imag, imag * tw_real + real * tw_imag], axis=0
    )
    return table_left(last, turned)


MESH_ID = pl.DeviceIdType.MESH
WINDOW = 2
AHEAD = 2
LOW_LAG = 1
OUT_PARTS = 4
RELAY_LAG = 2


def flip(index, mask):
    bit = 1
    while bit <= mask:
        if mask & bit:
            index = index + bit - 2 * bit * ((index // bit) % 2)
        bit *= 2
    return index


def plan(bands, per_band):
    upper = (3 * bands) // 8
    lower = bands - upper
    up = [("up", k) for k in range(upper)]
    down = [("down", k) for k in range(lower)]
    on_low, on_high = [], []
    for k in range(lower):
        on_low.append(down[k])
        on_low += up[k:k + 1]
    on_high = up[:2] + down[:1] + up[2:] + down[1:]
    low_steps, high_steps = lower * per_band, upper * per_band
    low_at = [(2 + n) if per_band == 2 else (n + 3) // 2 for n in range(bands)]
    low_at = [at + LOW_LAG if at + LOW_LAG < low_steps else None for at in low_at]
    high_at = [per_band * m for m in (1, 2)] + [high_steps - 1]
    high_at = [high_at[n] if n < len(high_at) else None for n in range(bands)]
    return upper, {True: list(zip(on_low, low_at)), False: list(zip(on_high, high_at))}


def layer_kernel(groups, chans, bands, *refs):
    (signal_h, response_h, gating_h, skip_h, weight_h, first_h, twiddle_h, second_h, last_h, hfirst_h, htwiddle_h, hlast_h,
     out_h,
     signal, response, gating, skip, first, twiddle, second, last, hfirst, htwiddle, hlast,
     send, held, hheld, made, hmade, conv, mixed, wall, wperm, wturn, *shares, out,
     dn_send, dn_recv, up_send, up_recv, lo_send, lo_recv, dback_send, dback_recv, uback_send, uback_recv,
     sib_send, sib_recv, row_send, row_recv, rel_send, rel_recv, w_send, w_recv, load_sem, out_sem, credit) = refs
    half = groups // 2
    per_band = 8 // half
    n_up, orders = plan(bands, per_band)
    n_down = bands - n_up
    cuts = [0, bands // 2, bands - 1, bands]
    up_steps, down_steps = n_up * per_band, n_down * per_band
    credits = max(down_steps - WINDOW, 0)
    tiles_in = signal.shape[1]
    samples = tiles_in * 128
    pieces = samples // INNER
    size = 2 * pieces
    chips = chans // 2
    chan_rows = bands * 8
    me = lax.axis_index("seq")
    mine = lax.axis_index("chan")
    chip, core = mine // 2, mine % 2
    sibling = chip * 2 + 1 - core
    low = me < half
    spot = me % half
    out_rows = out.shape[0]
    near = list(range(1, half))
    far = list(range(half, groups))

    def row_band(kind, k):
        return k if kind == "down" else n_down + k

    own_weights = wall.at[pl.ds(pl.multiple_of(mine * chan_rows, 8), chan_rows), :]

    loads = []
    for kind, k in [("down", 0), ("up", 0)] + [("down", k) for k in range(1, n_down)] + [("up", k) for k in range(1, n_up)]:
        b = row_band(kind, k)
        for src, dst in ((signal_h, signal), (response_h, response)):
            loads.append((src.at[b], dst.at[b], b))
    for src, dst in ((first_h, first), (twiddle_h, twiddle), (second_h, second), (last_h, last), (hfirst_h, hfirst),
                     (htwiddle_h, htwiddle), (hlast_h, hlast), (weight_h, own_weights), (skip_h, skip), (gating_h, gating)):
        loads.append((src, dst, -1))
    copies = [(pltpu.make_async_copy(src, dst, load_sem.at[n]), b) for n, (src, dst, b) in enumerate(loads)]

    barrier = pltpu.get_barrier_semaphore()
    for mask in range(1, groups):
        pl.semaphore_signal(barrier, inc=1, device_id={"seq": flip(me, mask)}, device_id_type=MESH_ID)
    for off in range(1, chans):
        pl.semaphore_signal(barrier, inc=1, device_id={"chan": lax.rem(mine + off, chans)}, device_id_type=MESH_ID)
    for copy, _ in copies:
        copy.start()

    def prepare(b):
        for r in range(8):
            for place, ref in enumerate((signal, response)):
                for side in range(2):
                    send[b, r, place, :, side * 128:(side + 1) * 128] = ref[b, pl.ds(side, pieces, stride=2), r, :]

    def source(step, base, who):
        return send.at[base + step // per_band, (step % per_band) * half + who % half]

    def copy_to(src, dst, send_sem, recv_sem, mask):
        return pltpu.make_async_remote_copy(
            src, dst, send_sem, recv_sem, device_id={"seq": flip(me, mask)}, device_id_type=MESH_ID)

    def down(step, mask):
        return copy_to(source(step, 0, flip(me, mask)), held.at[step * groups + me], dn_send.at[0], dn_recv.at[step], mask)

    def down_own(step):
        return pltpu.make_async_copy(source(step, 0, me), held.at[step * groups + me], dn_recv.at[step])

    def up(step, mask):
        return copy_to(source(step, n_down, flip(me, mask)), held.at[step * groups + me], up_send.at[0], up_recv.at[step], mask)

    def up_own(step):
        return pltpu.make_async_copy(source(step, n_down, me), held.at[step * groups + me], up_recv.at[step])

    def lower(step, mask):
        return copy_to(source(step, n_down, flip(me, mask)), hheld.at[step * half + me], lo_send.at[0], lo_recv.at[step], mask)

    def lower_own(step):
        return pltpu.make_async_copy(source(step, n_down, me), hheld.at[step * half + me], lo_recv.at[step])

    def made_rows(ref, width, step, who):
        return ref.at[pl.ds(pl.multiple_of((step * width + who) * size, size), size), :]

    def conv_rows(base, step):
        row = (base + step // per_band) * 8 + (step % per_band) * half + spot
        return conv.at[pl.ds(pl.multiple_of(row * size, size), size), :]

    def down_back(step, mask):
        return copy_to(made_rows(made, groups, step, flip(me, mask)), conv_rows(0, step),
                       dback_send.at[0], dback_recv.at[step // per_band], mask)

    def down_back_own(step):
        return pltpu.make_async_copy(made_rows(made, groups, step, me), conv_rows(0, step), dback_recv.at[step // per_band])

    def up_back(ref, width, step, mask):
        return copy_to(made_rows(ref, width, step, flip(me, mask)), conv_rows(n_down, step),
                       uback_send.at[0], uback_recv.at[step // per_band], mask)

    def up_back_own(ref, width, step):
        return pltpu.make_async_copy(made_rows(ref, width, step, me), conv_rows(n_down, step), uback_recv.at[step // per_band])

    def settle(ref, sem):
        pltpu.make_async_copy(ref, ref, sem).wait()

    def settle_sent(blocks, rows, sem):
        settle(held.at[pl.ds(0, blocks)] if rows is None else made.at[pl.ds(0, blocks * rows)], sem)

    def convolve(step, lowest):
        rows = held[pl.ds(step * groups, groups)]
        result = conv_row(
            rows[:, 0].reshape(groups * pieces, INNER), rows[:, 1].reshape(groups * pieces, INNER),
            first, twiddle, second, last)
        for g in range(lowest, groups):
            for side in range(2):
                start = pl.multiple_of(((step * groups + g) * 2 + side) * pieces, pieces)
                made[pl.ds(start, pieces), :] = result[g * pieces:(g + 1) * pieces, side * 128:(side + 1) * 128]

    def convolve_lower(step):
        rows = hheld[pl.ds(step * half, half)]
        result = conv_row(
            rows[:, 0].reshape(half * pieces, INNER), rows[:, 1].reshape(half * pieces, INNER),
            hfirst, htwiddle, second, hlast)
        for g in range(half):
            for side in range(2):
                start = pl.multiple_of(((step * half + g) * 2 + side) * pieces, pieces)
                hmade[pl.ds(start, pieces), :] = result[g * pieces:(g + 1) * pieces, side * 128:(side + 1) * 128]

    def chunk(pos, who, part):
        if pos < bands - 1:
            return mixed.at[pos * chans + who]
        return mixed.at[pos * chans + who, pl.ds(part * tiles_in // OUT_PARTS, tiles_in // OUT_PARTS)]

    def parts_of(pos):
        return range(OUT_PARTS if pos == bands - 1 else 1)

    def to_sibling(pos, part):
        return pltpu.make_async_remote_copy(
            chunk(pos, mine, part), chunk(pos, mine, part), sib_send.at[0], sib_recv.at[pos + part],
            device_id={"chan": sibling}, device_id_type=MESH_ID)

    def to_chip(pos, off, part):
        return pltpu.make_async_remote_copy(
            chunk(pos, mine, part), chunk(pos, mine, part), row_send.at[off - 1], row_recv.at[pos + part, off - 1],
            device_id={"chan": lax.rem(chip + off, chips) * 2 + core}, device_id_type=MESH_ID)

    def relay(pos, off, part):
        who = lax.rem(chip + chips - off, chips) * 2 + core
        return pltpu.make_async_remote_copy(
            chunk(pos, who, part), chunk(pos, who, part), rel_send.at[off - 1], rel_recv.at[pos + part, off - 1],
            device_id={"chan": sibling}, device_id_type=MESH_ID)

    def weights(off):
        return pltpu.make_async_remote_copy(
            own_weights, own_weights, w_send.at[off - 1], w_recv.at[off - 1],
            device_id={"chan": lax.rem(mine + off, chans)}, device_id_type=MESH_ID)

    def gate(pos, is_low):
        kind, k = orders[is_low][pos][0]
        b = row_band(kind, k)
        settle(conv.at[pl.ds(b * 8 * size, 8 * size), :], (dback_recv if kind == "down" else uback_recv).at[k])
        gain = gains[b * 8:(b + 1) * 8]
        share_tiles = tiles_in // len(parts_of(pos))
        for part in parts_of(pos):
            for tile in range(part * share_tiles, (part + 1) * share_tiles):
                start = b * 8 * size + (tile % 2) * pieces + tile // 2
                mixed[pos * chans + mine, tile] = gating[b, tile] * (
                    conv[pl.ds(start, 8, stride=size), :] + gain * signal[b, tile])
            for off in range(1, chips):
                to_chip(pos, off, part).start()
            to_sibling(pos, part).start()

    def pass_on(pos, part=0):
        for off in range(1, chips):
            to_chip(pos, off, part).wait_recv()
            relay(pos, off, part).start()

    def launch_down(step, is_low):
        for mask in (near if is_low else far):
            down(step, mask).start()
        if is_low:
            down_own(step).start()

    def launch_up(step, is_low):
        for mask in (far if is_low else near):
            up(step, mask).start()
        if is_low:
            for mask in near:
                lower(step, mask).start()
            lower_own(step).start()
        else:
            up_own(step).start()

    def wait_loads(b):
        for copy, which in copies:
            if which == b:
                copy.wait()

    def ready_band(kind, step):
        base = 0 if kind == "down" else n_down
        @pl.when(step % per_band == 0)
        def _():
            prepare(base + step // per_band)

    started = {"down": 0, "up": 0}
    first_steps = {"down": min(WINDOW, down_steps), "up": min(AHEAD, up_steps)}
    for kind, base in (("down", 0), ("up", n_down)):
        for k in range((first_steps[kind] + per_band - 1) // per_band):
            wait_loads(base + k)
            prepare(base + k)
            started[kind] = k + 1
    pl.semaphore_wait(barrier, groups + chans - 2)

    @pl.when(low)
    def _():
        for step in range(max(first_steps.values())):
            if step < first_steps["up"]:
                launch_up(step, True)
            if step < first_steps["down"]:
                launch_down(step, True)

    @pl.when(jnp.logical_not(low))
    def _():
        for step in range(first_steps["down"]):
            launch_down(step, False)
        for step in range(first_steps["up"]):
            launch_up(step, False)

    for kind, base, count in (("down", 0, n_down), ("up", n_down, n_up)):
        for k in range(started[kind], count):
            wait_loads(base + k)
            prepare(base + k)
    wait_loads(-1)
    for off in range(1, chans):
        weights(off).start()
    row = lax.broadcasted_iota(jnp.int32, (chan_rows, chan_rows), 0)
    col = lax.broadcasted_iota(jnp.int32, (chan_rows, chan_rows), 1)
    spread = jnp.where(row == col, jnp.broadcast_to(skip[...], (chan_rows, chan_rows)), 0.0)
    gains = jnp.broadcast_to(jnp.sum(spread, axis=1, keepdims=True), (chan_rows, 128))

    def share_weights():
        for off in range(1, chans):
            weights(off).wait()
        for pos in range(bands):
            here = [row_band(*orders[side][pos][0]) for side in (True, False)]
            b = jnp.where(low, here[0], here[1])
            for who in range(chans):
                wperm[pl.ds((pos * chans + who) * 8, 8), :] = wall[
                    pl.ds(pl.multiple_of((who * bands + b) * 8, 8), 8), :]
        for share, (lo, hi) in zip(shares, zip(cuts[:-1], cuts[1:])):
            width = (hi - lo) * chans * 8
            wturn[:, :width] = jnp.transpose(wperm[lo * chans * 8:hi * chans * 8, :])
            w_high, w_low = split(wturn[pl.ds(pl.multiple_of(mine * out_rows, 8), out_rows), :width])
            share[...] = jnp.concatenate([w_high, w_low], axis=0)

    def mix(n):
        lo, hi = cuts[n], cuts[n + 1]
        last_one = n == len(cuts) - 2
        depth = (hi - lo) * chans * 8
        parts = OUT_PARTS if last_one else 1
        if last_one:
            pass_on(lo, 0)
        for part in range(parts):
            if last_one and part + 1 < parts:
                pass_on(lo, part + 1)
            for pos in range(lo, hi):
                to_sibling(pos, part).wait_recv()
                for off in range(1, chips):
                    relay(pos, off, part).wait_recv()

            @pl.loop(part * (pieces // parts), (part + 1) * (pieces // parts))
            def _(i):
                data = jnp.concatenate(
                    [mixed[lo * chans:hi * chans, 2 * i + side].reshape(depth, 128) for side in range(2)], axis=1)
                high, low_part = split(data)
                weight_both = shares[n][...]
                both = matmul(weight_both, high)
                here = pl.ds(pl.multiple_of(i * INNER, INNER), INNER)
                total = both[:out_rows] + both[out_rows:] + matmul(weight_both[:out_rows], low_part)
                out[:, here] = total if n == 0 else out[:, here] + total
            if parts > 1:
                here = pl.ds(part * (samples // parts), samples // parts)
                pltpu.make_async_copy(out.at[:, here], out_h.at[:, here], out_sem.at[0]).start()

    def finish():
        for pos in range(bands - RELAY_LAG, bands - 1):
            pass_on(pos)
        mix(1)
        mix(2)

    def gates(first_pos, last_pos, is_low):
        for pos in range(first_pos, last_pos):
            gate(pos, is_low)
            if pos >= RELAY_LAG:
                pass_on(pos - RELAY_LAG)

    def run(is_low):
        at = [where for _, where in orders[is_low]]
        rest = at.index(None)
        steps = down_steps if is_low else up_steps

        @pl.loop(0, steps)
        def _(s):
            if is_low:
                settle(held.at[pl.ds(s * groups, groups)], dn_recv.at[s])

                @pl.when(s < credits)
                def _():
                    for mask in far:
                        pl.semaphore_signal(credit.at[s], inc=1, device_id={"seq": flip(me, mask)}, device_id_type=MESH_ID)

                @pl.when(s + AHEAD < up_steps)
                def _():
                    launch_up(s + AHEAD, True)

                @pl.when(s + WINDOW < down_steps)
                def _():
                    launch_down(s + WINDOW, True)

                convolve(s, 0)
                down_back_own(s).start()
                for mask in far + near:
                    down_back(s, mask).start()

                @pl.when(s < up_steps)
                def _():
                    settle(hheld.at[pl.ds(s * half, half)], lo_recv.at[s])
                    convolve_lower(s)
                    for mask in near:
                        up_back(hmade, half, s, mask).start()
                    up_back_own(hmade, half, s).start()
            else:
                @pl.when((s > 0) & (s - 1 < credits))
                def _():
                    pl.semaphore_wait(credit.at[s - 1], half)
                    launch_down(s - 1 + WINDOW, False)

                settle(held.at[pl.ds(s * groups, groups)], up_recv.at[s])

                @pl.when(s + AHEAD < up_steps)
                def _():
                    launch_up(s + AHEAD, False)

                convolve(s, half)
                for mask in near:
                    up_back(made, groups, s, mask).start()
                up_back_own(made, groups, s).start()

            @pl.when(s == 1)
            def _():
                share_weights()

            for where in sorted(set(at[:rest])):
                @pl.when(s == where)
                def _(where=where):
                    gates(at.index(where), at.index(where) + at.count(where), is_low)

        if not is_low:
            for s in range(up_steps - 1, credits):
                pl.semaphore_wait(credit.at[s], half)
                launch_down(s + WINDOW, False)
        gates(rest, cuts[2], is_low)
        mix(0)
        sends = ((down_steps * len(near if is_low else far), None, dn_send),
                 (up_steps * len(far if is_low else near), None, up_send),
                 (up_steps * len(near), size, uback_send))
        if is_low:
            sends += ((up_steps * len(near), None, lo_send), (down_steps * len(near + far), size, dback_send))
        gates(cuts[2], bands, is_low)
        finish()
        for blocks, rows, sem in sends:
            settle_sent(blocks, rows, sem.at[0])

    @pl.when(low)
    def _():
        run(True)

    @pl.when(jnp.logical_not(low))
    def _():
        run(False)

    settle(out, out_sem.at[0])
    settle(mixed.at[pl.ds(0, bands)], sib_send.at[0])
    for off in range(1, chips):
        settle(mixed.at[pl.ds(0, bands)], row_send.at[off - 1])
        settle(mixed.at[pl.ds(0, bands)], rel_send.at[off - 1])


def tiles(value):
    rows, columns = value.shape
    return value.reshape(rows // 8, 8, columns // 128, 128).transpose(0, 2, 1, 3)


def per_device(signal, gating, response, skip_gain, mixing_weight):
    chan_rows, samples = signal.shape
    groups = lax.axis_size("seq")
    chans = lax.axis_size("chan")
    half = groups // 2
    bands = chan_rows // 8
    per_band = 8 // half
    pieces = samples // INNER
    size = 2 * pieces
    chips = chans // 2
    depth = mixing_weight.shape[0]
    out_rows = depth // chans
    n_up, _ = plan(bands, per_band)
    up_steps, down_steps = n_up * per_band, (bands - n_up) * per_band
    slots = max(up_steps, down_steps)
    consts = [jnp.asarray(t) for t in tables(groups * samples)]
    hfirst, htwiddle, _, hlast = [jnp.asarray(t) for t in tables(half * samples)]
    consts += [hfirst, htwiddle, hlast]
    args = [tiles(signal), tiles(response), tiles(gating), skip_gain.reshape(1, chan_rows), mixing_weight.T, *consts]
    f32 = jnp.float32
    sems = pltpu.SemaphoreType.DMA
    anywhere = pl.BlockSpec(memory_space=pl.ANY)
    like = [args[0], args[1], args[2], args[3], *consts]
    n_loads = 2 * bands + len(args) - 2
    return pl.pallas_call(
        partial(layer_kernel, groups, chans, bands),
        in_specs=[anywhere] * len(args),
        out_specs=anywhere,
        out_shape=jax.ShapeDtypeStruct((out_rows, samples), f32),
        scratch_shapes=[pltpu.VMEM(a.shape, a.dtype) for a in like] + [
            pltpu.VMEM((bands, 8, 2, pieces, INNER), f32),
            pltpu.VMEM((slots * groups, 2, pieces, INNER), f32),
            pltpu.VMEM((up_steps * half, 2, pieces, INNER), f32),
            pltpu.VMEM((slots * groups * size, 128), f32),
            pltpu.VMEM((up_steps * half * size, 128), f32),
            pltpu.VMEM((chan_rows * size, 128), f32),
            pltpu.VMEM((bands * chans, samples // 128, 8, 128), f32),
            pltpu.VMEM((chans * chan_rows, depth), f32),
            pltpu.VMEM((chans * chan_rows, depth), f32),
            pltpu.VMEM((depth, chans * chan_rows // 2), f32),
            *[pltpu.VMEM((2 * out_rows, n * chans * 8), jnp.bfloat16) for n in (bands // 2, bands // 2 - 1, 1)],
            pltpu.VMEM((out_rows, samples), f32),
            sems((1,)), sems((down_steps,)),
            sems((1,)), sems((up_steps,)),
            sems((1,)), sems((up_steps,)),
            sems((1,)), sems((bands - n_up,)),
            sems((1,)), sems((n_up,)),
            sems((1,)), sems((bands - 1 + OUT_PARTS,)),
            sems((chips - 1,)), sems((bands - 1 + OUT_PARTS, chips - 1)),
            sems((chips - 1,)), sems((bands - 1 + OUT_PARTS, chips - 1)),
            sems((chans - 1,)), sems((chans - 1,)),
            sems((n_loads,)), sems((1,)),
            pltpu.SemaphoreType.REGULAR((down_steps,)),
        ],
        compiler_params=pltpu.CompilerParams(
            collective_id=0, has_side_effects=True, vmem_limit_bytes=62 * 2**20
        ),
        name="layer",
    )(*args)


def solution(mesh):
    in_specs = (P("chan", "seq"), P("chan", "seq"), P("chan", "seq"), P("chan"), P(None, "chan"))
    out_specs = P("chan", "seq")
    return jax.shard_map(
        per_device, mesh=mesh, in_specs=in_specs, out_specs=out_specs, check_vma=False
    )
```

```python
from functools import partial
import math

import jax
import jax.numpy as jnp
import numpy as np
from jax import lax
from jax.experimental import pallas as pl
from jax.experimental.pallas import tpu as pltpu
from jax.sharding import PartitionSpec as P

INNER = 256


def halves(table):
    high = np.asarray(table, np.float32).astype(jnp.bfloat16)
    low = (np.asarray(table, np.float64) - high.astype(np.float64)).astype(np.float32).astype(jnp.bfloat16)
    return high, low


def split(value):
    high = value.astype(jnp.bfloat16)
    return high, (value - high.astype(jnp.float32)).astype(jnp.bfloat16)


def tables(span):
    outer = span // INNER
    step_out = np.arange(outer, dtype=np.float64)
    step_in = np.arange(INNER, dtype=np.float64)
    angle = 2 * np.pi * np.mod((4 * step_out[:, None] + 1) * step_out[None, :], 4 * outer) / (4 * outer)
    cos_out, sin_out = np.cos(angle), -np.sin(angle)
    first = np.concatenate(halves(np.concatenate([cos_out, sin_out], axis=0)), axis=1)
    angle = 2 * np.pi * np.mod((4 * step_out[:, None] + 1) * step_in[None, :], 4 * span) / (4 * span)
    twiddle = np.stack([np.cos(angle), -np.sin(angle)]).astype(np.float32)
    angle = 2 * np.pi * np.mod(step_in[:, None] * step_in[None, :], INNER) / INNER
    cos_in, sin_in = np.cos(angle), -np.sin(angle)
    second = np.concatenate(halves(np.block([[cos_in, sin_in], [-sin_in, cos_in]])), axis=0)
    last = np.concatenate(halves(np.concatenate([cos_out.T, -sin_out.T], axis=1) / span), axis=1)
    return first, twiddle, second, last


def matmul(left, right):
    return jnp.dot(left, right, preferred_element_type=jnp.float32)


def table_left(table, value):
    high, low = split(value)
    depth = value.shape[0]
    return matmul(table[...], jnp.concatenate([high, high], axis=0)) + matmul(table[:, :depth], low)


def table_right(value, table):
    high, low = split(value)
    depth = value.shape[1]
    return matmul(jnp.concatenate([high, high], axis=1), table[...]) + matmul(low, table[:depth, :])


def conv_row(signal, response, first, twiddle, second, last):
    outer = signal.shape[0]
    mid = table_left(first, jnp.concatenate([signal, response], axis=1))
    tw_real, tw_imag = twiddle[0], twiddle[1]
    turned = []
    for place in range(2):
        cols = slice(place * INNER, (place + 1) * INNER)
        real, imag = mid[:outer, cols], mid[outer:, cols]
        turned.append(jnp.concatenate(
            [real * tw_real - imag * tw_imag, real * tw_imag + imag * tw_real], axis=1
        ))
    spectra = table_right(jnp.concatenate(turned, axis=0), second)
    s_real, s_imag = spectra[:outer, :INNER], spectra[:outer, INNER:]
    r_real, r_imag = spectra[outer:, :INNER], spectra[outer:, INNER:]
    prod = jnp.concatenate(
        [s_real * r_real - s_imag * r_imag, -(s_real * r_imag + s_imag * r_real)], axis=1
    )
    back = table_right(prod, second)
    real, imag = back[:, :INNER], back[:, INNER:]
    turned = jnp.concatenate(
        [real * tw_real - imag * tw_imag, imag * tw_real + real * tw_imag], axis=0
    )
    return table_left(last, turned)


MESH_ID = pl.DeviceIdType.MESH
WINDOW = 2
AHEAD = 2
LOW_LAG = 1
OUT_PARTS = 8
RELAY_LAG = 2


def flip(index, mask):
    bit = 1
    while bit <= mask:
        if mask & bit:
            index = index + bit - 2 * bit * ((index // bit) % 2)
        bit *= 2
    return index


def plan(bands, per_band):
    upper = (3 * bands) // 8
    lower = bands - upper
    up = [("up", k) for k in range(upper)]
    down = [("down", k) for k in range(lower)]
    on_low, on_high = [], []
    for k in range(lower):
        on_low.append(down[k])
        on_low += up[k:k + 1]
    on_high = up[:2] + down[:1] + up[2:] + down[1:]
    low_steps, high_steps = lower * per_band, upper * per_band
    low_at = [(2 + n) if per_band == 2 else (n + 3) // 2 for n in range(bands)]
    low_at = [at + LOW_LAG if at + LOW_LAG < low_steps else None for at in low_at]
    high_at = [per_band * m for m in (1, 2)] + [high_steps - 1]
    high_at = [high_at[n] if n < len(high_at) else None for n in range(bands)]
    return upper, {True: list(zip(on_low, low_at)), False: list(zip(on_high, high_at))}


def layer_kernel(groups, chans, bands, *refs):
    (signal_h, response_h, gating_h, skip_h, weight_h, first_h, twiddle_h, second_h, last_h, hfirst_h, htwiddle_h, hlast_h,
     out_h,
     signal, response, gating, skip, first, twiddle, second, last, hfirst, htwiddle, hlast,
     send, held, hheld, made, hmade, conv, mixed, wall, wperm, wturn, *shares, out,
     dn_send, dn_recv, up_send, up_recv, lo_send, lo_recv, dback_send, dback_recv, uback_send, uback_recv,
     sib_send, sib_recv, row_send, row_recv, rel_send, rel_recv, w_send, w_recv, load_sem, out_sem, credit) = refs
    half = groups // 2
    per_band = 8 // half
    n_up, orders = plan(bands, per_band)
    n_down = bands - n_up
    cuts = [0, bands // 2, bands - 1, bands]
    up_steps, down_steps = n_up * per_band, n_down * per_band
    credits = max(down_steps - WINDOW, 0)
    tiles_in = signal.shape[1]
    samples = tiles_in * 128
    pieces = samples // INNER
    size = 2 * pieces
    chips = chans // 2
    chan_rows = bands * 8
    me = lax.axis_index("seq")
    mine = lax.axis_index("chan")
    chip, core = mine // 2, mine % 2
    sibling = chip * 2 + 1 - core
    low = me < half
    spot = me % half
    out_rows = out.shape[0]
    near = list(range(1, half))
    far = list(range(half, groups))

    def row_band(kind, k):
        return k if kind == "down" else n_down + k

    own_weights = wall.at[pl.ds(pl.multiple_of(mine * chan_rows, 8), chan_rows), :]

    loads = []
    for kind, k in [("down", 0), ("up", 0)] + [("down", k) for k in range(1, n_down)] + [("up", k) for k in range(1, n_up)]:
        b = row_band(kind, k)
        for src, dst in ((signal_h, signal), (response_h, response)):
            loads.append((src.at[b], dst.at[b], b))
    for src, dst in ((first_h, first), (twiddle_h, twiddle), (second_h, second), (last_h, last), (hfirst_h, hfirst),
                     (htwiddle_h, htwiddle), (hlast_h, hlast), (weight_h, own_weights), (skip_h, skip), (gating_h, gating)):
        loads.append((src, dst, -1))
    copies = [(pltpu.make_async_copy(src, dst, load_sem.at[n]), b) for n, (src, dst, b) in enumerate(loads)]

    barrier = pltpu.get_barrier_semaphore()
    for mask in range(1, groups):
        pl.semaphore_signal(barrier, inc=1, device_id={"seq": flip(me, mask)}, device_id_type=MESH_ID)
    for off in range(1, chans):
        pl.semaphore_signal(barrier, inc=1, device_id={"chan": lax.rem(mine + off, chans)}, device_id_type=MESH_ID)
    for copy, _ in copies:
        copy.start()

    def prepare(b):
        for r in range(8):
            for place, ref in enumerate((signal, response)):
                for side in range(2):
                    send[b, r, place, :, side * 128:(side + 1) * 128] = ref[b, pl.ds(side, pieces, stride=2), r, :]

    def source(step, base, who):
        return send.at[base + step // per_band, (step % per_band) * half + who % half]

    def copy_to(src, dst, send_sem, recv_sem, mask):
        return pltpu.make_async_remote_copy(
            src, dst, send_sem, recv_sem, device_id={"seq": flip(me, mask)}, device_id_type=MESH_ID)

    def down(step, mask):
        return copy_to(source(step, 0, flip(me, mask)), held.at[step * groups + me], dn_send.at[0], dn_recv.at[step], mask)

    def down_own(step):
        return pltpu.make_async_copy(source(step, 0, me), held.at[step * groups + me], dn_recv.at[step])

    def up(step, mask):
        return copy_to(source(step, n_down, flip(me, mask)), held.at[step * groups + me], up_send.at[0], up_recv.at[step], mask)

    def up_own(step):
        return pltpu.make_async_copy(source(step, n_down, me), held.at[step * groups + me], up_recv.at[step])

    def lower(step, mask):
        return copy_to(source(step, n_down, flip(me, mask)), hheld.at[step * half + me], lo_send.at[0], lo_recv.at[step], mask)

    def lower_own(step):
        return pltpu.make_async_copy(source(step, n_down, me), hheld.at[step * half + me], lo_recv.at[step])

    def made_rows(ref, width, step, who):
        return ref.at[pl.ds(pl.multiple_of((step * width + who) * size, size), size), :]

    def conv_rows(base, step):
        row = (base + step // per_band) * 8 + (step % per_band) * half + spot
        return conv.at[pl.ds(pl.multiple_of(row * size, size), size), :]

    def down_back(step, mask):
        return copy_to(made_rows(made, groups, step, flip(me, mask)), conv_rows(0, step),
                       dback_send.at[0], dback_recv.at[step // per_band], mask)

    def down_back_own(step):
        return pltpu.make_async_copy(made_rows(made, groups, step, me), conv_rows(0, step), dback_recv.at[step // per_band])

    def up_back(ref, width, step, mask):
        return copy_to(made_rows(ref, width, step, flip(me, mask)), conv_rows(n_down, step),
                       uback_send.at[0], uback_recv.at[step // per_band], mask)

    def up_back_own(ref, width, step):
        return pltpu.make_async_copy(made_rows(ref, width, step, me), conv_rows(n_down, step), uback_recv.at[step // per_band])

    def settle(ref, sem):
        pltpu.make_async_copy(ref, ref, sem).wait()

    def settle_sent(blocks, rows, sem):
        settle(held.at[pl.ds(0, blocks)] if rows is None else made.at[pl.ds(0, blocks * rows)], sem)

    def convolve(step, lowest):
        rows = held[pl.ds(step * groups, groups)]
        result = conv_row(
            rows[:, 0].reshape(groups * pieces, INNER), rows[:, 1].reshape(groups * pieces, INNER),
            first, twiddle, second, last)
        for g in range(lowest, groups):
            for side in range(2):
                start = pl.multiple_of(((step * groups + g) * 2 + side) * pieces, pieces)
                made[pl.ds(start, pieces), :] = result[g * pieces:(g + 1) * pieces, side * 128:(side + 1) * 128]

    def convolve_lower(step):
        rows = hheld[pl.ds(step * half, half)]
        result = conv_row(
            rows[:, 0].reshape(half * pieces, INNER), rows[:, 1].reshape(half * pieces, INNER),
            hfirst, htwiddle, second, hlast)
        for g in range(half):
            for side in range(2):
                start = pl.multiple_of(((step * half + g) * 2 + side) * pieces, pieces)
                hmade[pl.ds(start, pieces), :] = result[g * pieces:(g + 1) * pieces, side * 128:(side + 1) * 128]

    def chunk(pos, who, part):
        if pos < bands - 1:
            return mixed.at[pos * chans + who]
        return mixed.at[pos * chans + who, pl.ds(part * tiles_in // OUT_PARTS, tiles_in // OUT_PARTS)]

    def parts_of(pos):
        return range(OUT_PARTS if pos == bands - 1 else 1)

    def to_sibling(pos, part):
        return pltpu.make_async_remote_copy(
            chunk(pos, mine, part), chunk(pos, mine, part), sib_send.at[0], sib_recv.at[pos + part],
            device_id={"chan": sibling}, device_id_type=MESH_ID)

    def to_chip(pos, off, part):
        return pltpu.make_async_remote_copy(
            chunk(pos, mine, part), chunk(pos, mine, part), row_send.at[off - 1], row_recv.at[pos + part, off - 1],
            device_id={"chan": lax.rem(chip + off, chips) * 2 + core}, device_id_type=MESH_ID)

    def relay(pos, off, part):
        who = lax.rem(chip + chips - off, chips) * 2 + core
        return pltpu.make_async_remote_copy(
            chunk(pos, who, part), chunk(pos, who, part), rel_send.at[off - 1], rel_recv.at[pos + part, off - 1],
            device_id={"chan": sibling}, device_id_type=MESH_ID)

    def weights(off):
        return pltpu.make_async_remote_copy(
            own_weights, own_weights, w_send.at[off - 1], w_recv.at[off - 1],
            device_id={"chan": lax.rem(mine + off, chans)}, device_id_type=MESH_ID)

    def gate(pos, is_low):
        kind, k = orders[is_low][pos][0]
        b = row_band(kind, k)
        settle(conv.at[pl.ds(b * 8 * size, 8 * size), :], (dback_recv if kind == "down" else uback_recv).at[k])
        gain = gains[b * 8:(b + 1) * 8]
        share_tiles = tiles_in // len(parts_of(pos))
        for part in parts_of(pos):
            for tile in range(part * share_tiles, (part + 1) * share_tiles):
                start = b * 8 * size + (tile % 2) * pieces + tile // 2
                mixed[pos * chans + mine, tile] = gating[b, tile] * (
                    conv[pl.ds(start, 8, stride=size), :] + gain * signal[b, tile])
            for off in range(1, chips):
                to_chip(pos, off, part).start()
            to_sibling(pos, part).start()

    def pass_on(pos, part=0):
        for off in range(1, chips):
            to_chip(pos, off, part).wait_recv()
            relay(pos, off, part).start()

    def launch_down(step, is_low):
        for mask in (near if is_low else far):
            down(step, mask).start()
        if is_low:
            down_own(step).start()

    def launch_up(step, is_low):
        for mask in (far if is_low else near):
            up(step, mask).start()
        if is_low:
            for mask in near:
                lower(step, mask).start()
            lower_own(step).start()
        else:
            up_own(step).start()

    def wait_loads(b):
        for copy, which in copies:
            if which == b:
                copy.wait()

    def ready_band(kind, step):
        base = 0 if kind == "down" else n_down
        @pl.when(step % per_band == 0)
        def _():
            prepare(base + step // per_band)

    started = {"down": 0, "up": 0}
    first_steps = {"down": min(WINDOW, down_steps), "up": min(AHEAD, up_steps)}
    for kind, base in (("down", 0), ("up", n_down)):
        for k in range((first_steps[kind] + per_band - 1) // per_band):
            wait_loads(base + k)
            prepare(base + k)
            started[kind] = k + 1
    pl.semaphore_wait(barrier, groups + chans - 2)

    @pl.when(low)
    def _():
        for step in range(max(first_steps.values())):
            if step < first_steps["up"]:
                launch_up(step, True)
            if step < first_steps["down"]:
                launch_down(step, True)

    @pl.when(jnp.logical_not(low))
    def _():
        for step in range(first_steps["down"]):
            launch_down(step, False)
        for step in range(first_steps["up"]):
            launch_up(step, False)

    for kind, base, count in (("down", 0, n_down), ("up", n_down, n_up)):
        for k in range(started[kind], count):
            wait_loads(base + k)
            prepare(base + k)
    wait_loads(-1)
    for off in range(1, chans):
        weights(off).start()
    row = lax.broadcasted_iota(jnp.int32, (chan_rows, chan_rows), 0)
    col = lax.broadcasted_iota(jnp.int32, (chan_rows, chan_rows), 1)
    spread = jnp.where(row == col, jnp.broadcast_to(skip[...], (chan_rows, chan_rows)), 0.0)
    gains = jnp.broadcast_to(jnp.sum(spread, axis=1, keepdims=True), (chan_rows, 128))

    def share_weights():
        for off in range(1, chans):
            weights(off).wait()
        for pos in range(bands):
            here = [row_band(*orders[side][pos][0]) for side in (True, False)]
            b = jnp.where(low, here[0], here[1])
            for who in range(chans):
                wperm[pl.ds((pos * chans + who) * 8, 8), :] = wall[
                    pl.ds(pl.multiple_of((who * bands + b) * 8, 8), 8), :]
        for share, (lo, hi) in zip(shares, zip(cuts[:-1], cuts[1:])):
            width = (hi - lo) * chans * 8
            wturn[:, :width] = jnp.transpose(wperm[lo * chans * 8:hi * chans * 8, :])
            w_high, w_low = split(wturn[pl.ds(pl.multiple_of(mine * out_rows, 8), out_rows), :width])
            share[...] = jnp.concatenate([w_high, w_low], axis=0)

    def mix(n):
        lo, hi = cuts[n], cuts[n + 1]
        last_one = n == len(cuts) - 2
        depth = (hi - lo) * chans * 8
        parts = OUT_PARTS if last_one else 1
        if last_one:
            pass_on(lo, 0)
        for part in range(parts):
            if last_one and part + 1 < parts:
                pass_on(lo, part + 1)
            for pos in range(lo, hi):
                to_sibling(pos, part).wait_recv()
                for off in range(1, chips):
                    relay(pos, off, part).wait_recv()

            @pl.loop(part * (pieces // parts), (part + 1) * (pieces // parts))
            def _(i):
                data = jnp.concatenate(
                    [mixed[lo * chans:hi * chans, 2 * i + side].reshape(depth, 128) for side in range(2)], axis=1)
                high, low_part = split(data)
                weight_both = shares[n][...]
                both = matmul(weight_both, high)
                here = pl.ds(pl.multiple_of(i * INNER, INNER), INNER)
                total = both[:out_rows] + both[out_rows:] + matmul(weight_both[:out_rows], low_part)
                out[:, here] = total if n == 0 else out[:, here] + total
            if parts > 1:
                here = pl.ds(part * (samples // parts), samples // parts)
                pltpu.make_async_copy(out.at[:, here], out_h.at[:, here], out_sem.at[0]).start()

    def finish():
        for pos in range(bands - RELAY_LAG, bands - 1):
            pass_on(pos)
        mix(1)
        mix(2)

    def gates(first_pos, last_pos, is_low):
        for pos in range(first_pos, last_pos):
            gate(pos, is_low)
            if pos >= RELAY_LAG:
                pass_on(pos - RELAY_LAG)

    def run(is_low):
        at = [where for _, where in orders[is_low]]
        rest = at.index(None)
        steps = down_steps if is_low else up_steps

        @pl.loop(0, steps)
        def _(s):
            if is_low:
                settle(held.at[pl.ds(s * groups, groups)], dn_recv.at[s])

                @pl.when(s < credits)
                def _():
                    for mask in far:
                        pl.semaphore_signal(credit.at[s], inc=1, device_id={"seq": flip(me, mask)}, device_id_type=MESH_ID)

                @pl.when(s + AHEAD < up_steps)
                def _():
                    launch_up(s + AHEAD, True)

                @pl.when(s + WINDOW < down_steps)
                def _():
                    launch_down(s + WINDOW, True)

                convolve(s, 0)
                down_back_own(s).start()
                for mask in far + near:
                    down_back(s, mask).start()

                @pl.when(s < up_steps)
                def _():
                    settle(hheld.at[pl.ds(s * half, half)], lo_recv.at[s])
                    convolve_lower(s)
                    for mask in near:
                        up_back(hmade, half, s, mask).start()
                    up_back_own(hmade, half, s).start()
            else:
                @pl.when((s > 0) & (s - 1 < credits))
                def _():
                    pl.semaphore_wait(credit.at[s - 1], half)
                    launch_down(s - 1 + WINDOW, False)

                settle(held.at[pl.ds(s * groups, groups)], up_recv.at[s])

                @pl.when(s + AHEAD < up_steps)
                def _():
                    launch_up(s + AHEAD, False)

                convolve(s, half)
                for mask in near:
                    up_back(made, groups, s, mask).start()
                up_back_own(made, groups, s).start()

            @pl.when(s == 1)
            def _():
                share_weights()

            for where in sorted(set(at[:rest])):
                @pl.when(s == where)
                def _(where=where):
                    gates(at.index(where), at.index(where) + at.count(where), is_low)

        if not is_low:
            for s in range(up_steps - 1, credits):
                pl.semaphore_wait(credit.at[s], half)
                launch_down(s + WINDOW, False)
        gates(rest, cuts[2], is_low)
        mix(0)
        sends = ((down_steps * len(near if is_low else far), None, dn_send),
                 (up_steps * len(far if is_low else near), None, up_send),
                 (up_steps * len(near), size, uback_send))
        if is_low:
            sends += ((up_steps * len(near), None, lo_send), (down_steps * len(near + far), size, dback_send))
        gates(cuts[2], bands, is_low)
        finish()
        for blocks, rows, sem in sends:
            settle_sent(blocks, rows, sem.at[0])

    @pl.when(low)
    def _():
        run(True)

    @pl.when(jnp.logical_not(low))
    def _():
        run(False)

    settle(out, out_sem.at[0])
    settle(mixed.at[pl.ds(0, bands)], sib_send.at[0])
    for off in range(1, chips):
        settle(mixed.at[pl.ds(0, bands)], row_send.at[off - 1])
        settle(mixed.at[pl.ds(0, bands)], rel_send.at[off - 1])


def tiles(value):
    rows, columns = value.shape
    return value.reshape(rows // 8, 8, columns // 128, 128).transpose(0, 2, 1, 3)


def per_device(signal, gating, response, skip_gain, mixing_weight):
    chan_rows, samples = signal.shape
    groups = lax.axis_size("seq")
    chans = lax.axis_size("chan")
    half = groups // 2
    bands = chan_rows // 8
    per_band = 8 // half
    pieces = samples // INNER
    size = 2 * pieces
    chips = chans // 2
    depth = mixing_weight.shape[0]
    out_rows = depth // chans
    n_up, _ = plan(bands, per_band)
    up_steps, down_steps = n_up * per_band, (bands - n_up) * per_band
    slots = max(up_steps, down_steps)
    consts = [jnp.asarray(t) for t in tables(groups * samples)]
    hfirst, htwiddle, _, hlast = [jnp.asarray(t) for t in tables(half * samples)]
    consts += [hfirst, htwiddle, hlast]
    args = [tiles(signal), tiles(response), tiles(gating), skip_gain.reshape(1, chan_rows), mixing_weight.T, *consts]
    f32 = jnp.float32
    sems = pltpu.SemaphoreType.DMA
    anywhere = pl.BlockSpec(memory_space=pl.ANY)
    like = [args[0], args[1], args[2], args[3], *consts]
    n_loads = 2 * bands + len(args) - 2
    return pl.pallas_call(
        partial(layer_kernel, groups, chans, bands),
        in_specs=[anywhere] * len(args),
        out_specs=anywhere,
        out_shape=jax.ShapeDtypeStruct((out_rows, samples), f32),
        scratch_shapes=[pltpu.VMEM(a.shape, a.dtype) for a in like] + [
            pltpu.VMEM((bands, 8, 2, pieces, INNER), f32),
            pltpu.VMEM((slots * groups, 2, pieces, INNER), f32),
            pltpu.VMEM((up_steps * half, 2, pieces, INNER), f32),
            pltpu.VMEM((slots * groups * size, 128), f32),
            pltpu.VMEM((up_steps * half * size, 128), f32),
            pltpu.VMEM((chan_rows * size, 128), f32),
            pltpu.VMEM((bands * chans, samples // 128, 8, 128), f32),
            pltpu.VMEM((chans * chan_rows, depth), f32),
            pltpu.VMEM((chans * chan_rows, depth), f32),
            pltpu.VMEM((depth, chans * chan_rows // 2), f32),
            *[pltpu.VMEM((2 * out_rows, n * chans * 8), jnp.bfloat16) for n in (bands // 2, bands // 2 - 1, 1)],
            pltpu.VMEM((out_rows, samples), f32),
            sems((1,)), sems((down_steps,)),
            sems((1,)), sems((up_steps,)),
            sems((1,)), sems((up_steps,)),
            sems((1,)), sems((bands - n_up,)),
            sems((1,)), sems((n_up,)),
            sems((1,)), sems((bands - 1 + OUT_PARTS,)),
            sems((chips - 1,)), sems((bands - 1 + OUT_PARTS, chips - 1)),
            sems((chips - 1,)), sems((bands - 1 + OUT_PARTS, chips - 1)),
            sems((chans - 1,)), sems((chans - 1,)),
            sems((n_loads,)), sems((1,)),
            pltpu.SemaphoreType.REGULAR((down_steps,)),
        ],
        compiler_params=pltpu.CompilerParams(
            collective_id=0, has_side_effects=True, vmem_limit_bytes=62 * 2**20
        ),
        name="layer",
    )(*args)


def solution(mesh):
    in_specs = (P("chan", "seq"), P("chan", "seq"), P("chan", "seq"), P("chan"), P(None, "chan"))
    out_specs = P("chan", "seq")
    return jax.shard_map(
        per_device, mesh=mesh, in_specs=in_specs, out_specs=out_specs, check_vma=False
    )
```
